512 devices in a mesh: dp: 32 (over z_lo, x, core), tensor: 16 (over z_hi, y).
Axes of the slice: x: 4, y: 4, z: 16 (z_hi: 4, z_lo: 4; z = z_hi * 4 + z_lo), core: 2. Of those that a mesh axis runs over, the one named last changes fastest.
Arguments:
- inputs: bfloat16 [32768, 8192], P('dp', 'tensor'), may hold values from -6 to 6
- cotangent: bfloat16 [32768, 8192], P('dp', 'tensor'), may hold values from -6 to 6
- projector: bfloat16 [8192, 512], P('tensor'), may hold values from -0.0625 to 0.0625
- weight: bfloat16 [8192, 8192], P('dp', 'tensor'), may hold values from -6 to 6
- moment: float32 [512, 8192], P('dp', 'tensor'), may hold values from -6 to 6
- second_moment: float32 [512, 8192], P('dp', 'tensor'), may hold values from 0.01 to 1
Outputs:
- new_weight: bfloat16 [8192, 8192], P('dp', 'tensor')
- new_moment: float32 [512, 8192], P('dp', 'tensor')
- new_second: float32 [512, 8192], P('dp', 'tensor')
The draws below stay inside these ranges and needn't reach their ends.
All inputs are finite; a program needn't handle non-finite values.
Results may differ from the reference program's by a relative error of at most 0.0034.
Values may be sent and summed in bfloat16 or wider, within the bound.
No kernel may reach another device: no remote copies, remote signals or barrier semaphores. Data moves between devices by JAX's collectives and lax.ppermute only.
A program may use at most 64 MiB of HBM per device.

```python
import math
import jax
import jax.numpy as jnp

D = 8192
RANK = 512
STEP = 1000
TOKENS = 32768


def steps_of(own_key, shape, pieces, smallest, top_value):
    level = 1.0
    for dim, blocks in pieces:
        heights = jax.random.uniform(jax.random.fold_in(jax.random.fold_in(own_key, 6), dim), (blocks,), jnp.float32, smallest / len(pieces), top_value / len(pieces))
        level = level * jnp.repeat(jnp.exp(heights), shape[dim] // blocks).reshape((-1,) + (1,) * (len(shape) - 1 - dim))
    return level


def normal_values(own_key, extent, width, limit, shards=(), held_as=jnp.bfloat16):
    array = width * jax.random.normal(own_key, extent, jnp.float32)
    if shards:
        array = array * steps_of(own_key, extent, shards, -0.22, 0.18)
    return jnp.clip(array, -limit, limit).astype(held_as)


def setup_inputs(seed: int = 0) -> dict:
    splits = jax.random.split(jax.random.key(seed), 7)
    return {
        "inputs": normal_values(splits[0], (TOKENS, D), 1.0, 6.0, ((0, 32), (1, 16))),
        "cotangent": normal_values(splits[1], (TOKENS, D), 1.0, 6.0, ((0, 32), (1, 16))),
        "projector": normal_values(splits[2], (D, RANK), D ** -0.5, 0.0625, ((0, 16),)),
        "weight": normal_values(splits[3], (D, D), 1.0, 6.0, ((0, 32), (1, 16))),
        "moment": normal_values(splits[4], (RANK, D), 1.0, 6.0, ((0, 32), (1, 16)), jnp.float32),
        "second_moment": jnp.clip(jnp.exp(math.log(1.0) - 4.6051702 * jax.random.uniform(splits[5], (RANK, D), jnp.float32) ** steps_of(splits[5], (RANK, D), ((0, 32), (1, 16)), -0.2, 0.2)), 0.01, 1.0),
    }


beta_one = 0.9
beta_two = 0.999
epsilon = 1e-08
step_size = 0.5

def reference(inputs, cotangent, projector, weight, moment, second_moment):
    projected = jnp.dot(inputs, projector, preferred_element_type=jnp.float32).astype(jnp.bfloat16)
    gradient = jnp.dot(projected.T, cotangent, preferred_element_type=jnp.float32) * (1.0 / math.sqrt(TOKENS))
    new_moment = beta_one * moment + (1.0 - beta_one) * gradient
    new_second = beta_two * second_moment + (1.0 - beta_two) * gradient * gradient
    first_fix = 1.0 - beta_one ** STEP
    second_fix = 1.0 - beta_two ** STEP
    update = (new_moment / first_fix / (jnp.sqrt(new_second / second_fix) + epsilon)).astype(jnp.bfloat16)
    expanded = jnp.dot(projector, update, preferred_element_type=jnp.float32)
    new_weight = (weight.astype(jnp.float32) - step_size * expanded).astype(jnp.bfloat16)
    return (new_weight, new_moment, new_second)
```

```python
import math

import jax
import jax.numpy as jnp
from jax import lax
from jax.sharding import Mesh, PartitionSpec as P

STEP = 1000


beta_one = 0.9
beta_two = 0.999
epsilon = 1e-08
step_size = 0.5

DATA = ("zl", "x", "core")
MODEL = ("zh", "y")
SIZES = {"zl": 4, "x": 4, "core": 2, "zh": 4, "y": 4}
bf16 = jnp.bfloat16
f32 = jnp.float32


def exchange(parts, axis):
    return lax.all_to_all(parts, axis, 0, 0)


def spread(block, axis, count):
    return exchange(jnp.broadcast_to(block[None], (count,) + block.shape), axis)


def basis_rows(projector, rows):
    half = lax.dynamic_slice_in_dim(projector, lax.axis_index("core") * rows, rows, 0)
    pairs = []
    for zl in range(4):
        for x in range(4):
            for core in range(2):
                for zh in range(4):
                    for y in range(4):
                        source = (((zl * 4 + x) * 2 + core) * 4 + zh) * 4 + y
                        target = (((zh * 4 + y) * 2 + core) * 4 + zl) * 4 + x
                        pairs.append((source, target))
    return lax.ppermute(half, DATA + MODEL, pairs)


def on_device(inputs, cotangent, projector, weight, moment, second_moment):
    tokens, width = inputs.shape[0], cotangent.shape[1]
    rank = projector.shape[1]
    rows = weight.shape[0]
    own_rows = basis_rows(projector, rows)

    partial_sum = jnp.dot(inputs, projector, preferred_element_type=f32).astype(bf16)
    parts = exchange(partial_sum.reshape(4, tokens // 4, rank), "y")
    half_sum = jnp.sum(parts.astype(f32), axis=0).astype(bf16)
    parts = exchange(half_sum.reshape(4, tokens // 16, rank), "zh")
    owned = jnp.sum(parts.astype(f32), axis=0).astype(bf16)
    quarter = spread(owned, "zh", 4).reshape(tokens // 4, rank)
    projected = spread(quarter, "y", 4).reshape(tokens, rank)

    scale = 1.0 / math.sqrt(tokens * 32)
    partial_gradient = lax.dot_general(
        projected, cotangent, (((0,), (0,)), ((), ())), preferred_element_type=f32
    ).astype(bf16)
    parts = exchange(partial_gradient.reshape(32, rank // 32, width), DATA)
    gradient = jnp.sum(parts.astype(f32), axis=0) * scale
    new_moment = beta_one * moment + (1.0 - beta_one) * gradient
    new_second = beta_two * second_moment + (1.0 - beta_two) * gradient * gradient
    first_fix = 1.0 - beta_one**STEP
    second_fix = 1.0 - beta_two**STEP
    update = (new_moment / first_fix / (jnp.sqrt(new_second / second_fix) + epsilon)).astype(bf16)
    segment = spread(update, DATA, 32).reshape(rank, width)
    expanded = jnp.dot(own_rows, segment, preferred_element_type=f32)
    new_weight = (weight.astype(f32) - step_size * expanded).astype(bf16)
    return (new_weight, new_moment, new_second)


def solution(mesh):
    names = DATA + MODEL
    fine = Mesh(mesh.devices.reshape([SIZES[name] for name in names]), names)
    split = P(DATA, MODEL)
    return jax.shard_map(
        on_device,
        mesh=fine,
        in_specs=(split, split, P(MODEL, None), split, split, split),
        out_specs=(split, split, split),
        check_vma=False,
    )
```

```python
import math

import jax
import jax.numpy as jnp
from jax import lax
from jax.experimental.layout import Layout, with_layout_constraint
from jax.sharding import Mesh, PartitionSpec as P

STEP = 1000


beta_one = 0.9
beta_two = 0.999
epsilon = 1e-08
step_size = 0.5

DATA = ("zl", "x", "core")
PLANE = ("zl", "x")
MODEL = ("zh", "y")
SIZES = {"zl": 4, "x": 4, "core": 2, "zh": 4, "y": 4}
bf16 = jnp.bfloat16
f32 = jnp.float32


def exchange(parts, axis):
    return lax.all_to_all(parts, axis, 0, 0)


def spread(block, axis, count):
    return exchange(jnp.broadcast_to(block[None], (count,) + block.shape), axis)


def rowwise(array):
    return with_layout_constraint(array, Layout(major_to_minor=(0, 1)))


def total(parts):
    return jnp.sum(parts.astype(f32), axis=0)


def regrouped(projector):
    rank = projector.shape[1]
    new = lax.broadcasted_iota(jnp.int32, (rank, rank), 1)
    old = lax.broadcasted_iota(jnp.int32, (rank, rank), 0)
    source = ((new & 240) << 1) | ((new >> 8) << 4) | (new & 15)
    select = (old == source).astype(bf16)
    return jnp.dot(projector, select, preferred_element_type=f32).astype(bf16)


def basis_rows(basis, rows):
    half = lax.dynamic_slice_in_dim(basis, lax.axis_index("core") * rows, rows, 0)
    pairs = []
    for zl in range(4):
        for x in range(4):
            for core in range(2):
                for zh in range(4):
                    for y in range(4):
                        source = (((zl * 4 + x) * 2 + core) * 4 + zh) * 4 + y
                        target = (((zh * 4 + y) * 2 + core) * 4 + zl) * 4 + x
                        pairs.append((source, target))
    return lax.ppermute(half, DATA + MODEL, pairs)


def step(inputs, cotangent, projector, weight, moment, second_moment):
    tokens, width = inputs.shape[0], cotangent.shape[1]
    rank = projector.shape[1]
    rows = weight.shape[0]
    basis = regrouped(projector)
    own_rows = basis_rows(basis, rows)
    negative_rows = lax.optimization_barrier(-own_rows)

    partial_sum = rowwise(jnp.dot(inputs, basis, preferred_element_type=f32).astype(bf16))
    parts = exchange(partial_sum.reshape(4, tokens // 4, rank), "y")
    half_sum = total(parts).astype(bf16)
    parts = exchange(half_sum.reshape(4, tokens // 16, rank), "zh")
    owned = total(parts).astype(bf16)
    quarter = spread(owned, "zh", 4).reshape(tokens // 4, rank)
    projected = spread(quarter, "y", 4).reshape(tokens, rank)

    scale = 1.0 / math.sqrt(tokens * 32)
    partial_gradient = lax.dot_general(
        projected, cotangent, (((0,), (0,)), ((), ())), preferred_element_type=f32
    ).astype(bf16)
    parts = exchange(partial_gradient.reshape(2, rank // 2, width), "core")
    chip_gradient = total(parts).astype(bf16)
    parts = exchange(chip_gradient.reshape(16, rank // 32, width), PLANE)
    gradient = total(parts) * scale
    new_moment = beta_one * moment + (1.0 - beta_one) * gradient
    new_second = beta_two * second_moment + (1.0 - beta_two) * gradient * gradient
    first_fix = 1.0 - beta_one**STEP
    second_fix = 1.0 - beta_two**STEP
    update = (new_moment / first_fix / (jnp.sqrt(new_second / second_fix) + epsilon)).astype(bf16)
    segment = spread(update, PLANE, 16).reshape(rank // 2, width)
    segment = lax.all_gather(segment, "core", axis=0, tiled=True)
    negative = jnp.dot(negative_rows, segment, preferred_element_type=f32)
    new_weight = (weight.astype(f32) + step_size * negative).astype(bf16)
    return (new_weight, new_moment, new_second)


def solution(mesh):
    names = DATA + MODEL
    fine = Mesh(mesh.devices.reshape([SIZES[name] for name in names]), names)
    split = P(DATA, MODEL)
    return jax.shard_map(
        step,
        mesh=fine,
        in_specs=(split, split, P(MODEL, None), split, split, split),
        out_specs=(split, split, split),
        check_vma=False,
    )
```

```python
import math

import jax
import jax.numpy as jnp
from jax import lax
from jax.experimental.layout import Layout, with_layout_constraint
from jax.sharding import Mesh, PartitionSpec as P

STEP = 1000


beta_one = 0.9
beta_two = 0.999
epsilon = 1e-08
step_size = 0.5

DATA = ("zl", "x", "core")
PLANE = ("zl", "x")
MODEL = ("zh", "y")
SIZES = {"zl": 4, "x": 4, "core": 2, "zh": 4, "y": 4}
bf16 = jnp.bfloat16
f32 = jnp.float32


def exchange(parts, axis):
    return lax.all_to_all(parts, axis, 0, 0)


def spread(block, axis, count):
    return exchange(jnp.broadcast_to(block[None], (count,) + block.shape), axis)


def rowwise(array):
    return with_layout_constraint(array, Layout(major_to_minor=(0, 1)))


def total(parts):
    return jnp.sum(parts.astype(f32), axis=0)


def regrouped(projector):
    rank = projector.shape[1]
    new = lax.broadcasted_iota(jnp.int32, (rank, rank), 1)
    old = lax.broadcasted_iota(jnp.int32, (rank, rank), 0)
    source = ((new & 240) << 1) | ((new >> 8) << 4) | (new & 15)
    select = (old == source).astype(bf16)
    return jnp.dot(projector, select, preferred_element_type=f32).astype(bf16)


HOPS = ((0, 2, 3, 1), (0, 2, 3, 1), (2, 0, 1, 3), (2, 0, 1, 3))


def place(zl, x, core, zh, y):
    return (((zl * 4 + x) * 2 + core) * 4 + zh) * 4 + y


def moved(rows, source_of):
    pairs = []
    for zl in range(4):
        for x in range(4):
            for core in range(2):
                for zh in range(4):
                    for y in range(4):
                        here = (zl, x, core, zh, y)
                        pairs.append((place(*source_of(*here)), place(*here)))
    return lax.optimization_barrier(-lax.ppermute(rows, DATA + MODEL, pairs))


def basis_rows(basis, rows):
    half = lax.dynamic_slice_in_dim(basis, lax.axis_index("core") * rows, rows, 0)
    half = moved(half, lambda zl, x, core, zh, y: (HOPS[zl][zh], x, core, zl, y))
    half = moved(half, lambda zl, x, core, zh, y: (zl, x, core, zh, (y - x) % 4))
    half = moved(half, lambda zl, x, core, zh, y: (zl, (y - x) % 4, core, zh, y))
    return half


def step(inputs, cotangent, projector, weight, moment, second_moment):
    tokens, width = inputs.shape[0], cotangent.shape[1]
    rank = projector.shape[1]
    rows = weight.shape[0]
    basis = regrouped(projector)
    negative_rows = basis_rows(basis, rows)

    partial_sum = rowwise(jnp.dot(inputs, basis, preferred_element_type=f32).astype(bf16))
    parts = exchange(partial_sum.reshape(4, tokens // 4, rank), "y")
    half_sum = total(parts).astype(bf16)
    parts = exchange(half_sum.reshape(4, tokens // 16, rank), "zh")
    owned = total(parts).astype(bf16)
    quarter = spread(owned, "zh", 4).reshape(tokens // 4, rank)
    projected = spread(quarter, "y", 4).reshape(tokens, rank)

    scale = 1.0 / math.sqrt(tokens * 32)
    partial_gradient = lax.dot_general(
        projected, cotangent, (((0,), (0,)), ((), ())), preferred_element_type=f32
    ).astype(bf16)
    parts = exchange(partial_gradient.reshape(2, rank // 2, width), "core")
    chip_gradient = total(parts).astype(bf16)
    parts = exchange(chip_gradient.reshape(16, rank // 32, width), PLANE)
    gradient = total(parts) * scale
    new_moment = beta_one * moment + (1.0 - beta_one) * gradient
    new_second = beta_two * second_moment + (1.0 - beta_two) * gradient * gradient
    first_fix = 1.0 - beta_one**STEP
    second_fix = 1.0 - beta_two**STEP
    update = (new_moment / first_fix / (jnp.sqrt(new_second / second_fix) + epsilon)).astype(bf16)
    segment = spread(update, PLANE, 16).reshape(rank // 2, width)
    segment = lax.all_gather(segment, "core", axis=0, tiled=True)
    negative = jnp.dot(negative_rows, segment, preferred_element_type=f32)
    new_weight = (weight.astype(f32) + step_size * negative).astype(bf16)
    return (new_weight, new_moment, new_second)


def solution(mesh):
    names = DATA + MODEL
    fine = Mesh(mesh.devices.reshape([SIZES[name] for name in names]), names)
    split = P(DATA, MODEL)
    return jax.shard_map(
        step,
        mesh=fine,
        in_specs=(split, split, P(MODEL, None), split, split, split),
        out_specs=(split, split, split),
        check_vma=False,
    )
```

```python
import math

import jax
import jax.numpy as jnp
from jax import lax
from jax.experimental.layout import Layout, with_layout_constraint
from jax.sharding import Mesh, PartitionSpec as P

STEP = 1000


beta_one = 0.9
beta_two = 0.999
epsilon = 1e-08
step_size = 0.5

DATA = ("zl", "x", "core")
PLANE = ("zl", "x")
MODEL = ("zh", "y")
SIZES = {"zl": 4, "x": 4, "core": 2, "zh": 4, "y": 4}
bf16 = jnp.bfloat16
f32 = jnp.float32


def exchange(parts, axis):
    return lax.all_to_all(parts, axis, 0, 0)


def spread(block, axis, count):
    return exchange(jnp.broadcast_to(block[None], (count,) + block.shape), axis)


def rowwise(array):
    return with_layout_constraint(array, Layout(major_to_minor=(0, 1)))


def total(parts):
    return jnp.sum(parts.astype(f32), axis=0)


NEAR = (((0, 1), (1, 0), (2, 3), (3, 2)), ((0, 3), (3, 0), (1, 2), (2, 1)))


def line_sum(piece, first):
    for stage in range(2):
        other = lax.ppermute(piece, "zh", NEAR[(first + stage) % 2])
        piece = lax.optimization_barrier((piece.astype(f32) + other.astype(f32)).astype(bf16))
    return piece


def regrouped(projector):
    rank = projector.shape[1]
    new = lax.broadcasted_iota(jnp.int32, (rank, rank), 1)
    old = lax.broadcasted_iota(jnp.int32, (rank, rank), 0)
    source = ((new & 240) << 1) | ((new >> 8) << 4) | (new & 15)
    select = (old == source).astype(bf16)
    return jnp.dot(projector, select, preferred_element_type=f32).astype(bf16)


HOPS = ((0, 2, 3, 1), (0, 2, 3, 1), (2, 0, 1, 3), (2, 0, 1, 3))


def place(zl, x, core, zh, y):
    return (((zl * 4 + x) * 2 + core) * 4 + zh) * 4 + y


def moved(rows, source_of):
    pairs = []
    for zl in range(4):
        for x in range(4):
            for core in range(2):
                for zh in range(4):
                    for y in range(4):
                        here = (zl, x, core, zh, y)
                        pairs.append((place(*source_of(*here)), place(*here)))
    return lax.ppermute(rows, DATA + MODEL, pairs)


def basis_rows(basis, rows):
    half = lax.dynamic_slice_in_dim(basis, lax.axis_index("core") * rows, rows, 0)
    half = moved(half, lambda zl, x, core, zh, y: (zl, x, core, zh, (y - x) % 4))
    half = lax.optimization_barrier(-half)
    return moved(
        half, lambda zl, x, core, zh, y: (HOPS[zl][zh], (y - x) % 4, core, zl, y)
    )


def step(inputs, cotangent, projector, weight, moment, second_moment):
    tokens, width = inputs.shape[0], cotangent.shape[1]
    rank = projector.shape[1]
    rows = weight.shape[0]
    basis = regrouped(projector)
    negative_rows = basis_rows(basis, rows)

    partial_sum = rowwise(jnp.dot(inputs, basis, preferred_element_type=f32).astype(bf16))
    parts = exchange(partial_sum.reshape(4, tokens // 4, rank), "y")
    pieces = []
    for index in range(2):
        piece = parts[:, index * (tokens // 8) : (index + 1) * (tokens // 8)]
        piece = lax.optimization_barrier(total(piece).astype(bf16))
        pieces.append(line_sum(piece, index))
    quarter = jnp.concatenate(pieces)
    projected = spread(quarter, "y", 4).reshape(tokens, rank)

    scale = 1.0 / math.sqrt(tokens * 32)
    partial_gradient = lax.dot_general(
        projected, cotangent, (((0,), (0,)), ((), ())), preferred_element_type=f32
    ).astype(bf16)
    parts = exchange(partial_gradient.reshape(2, rank // 2, width), "core")
    chip_gradient = total(parts).astype(bf16)
    parts = exchange(chip_gradient.reshape(16, rank // 32, width), PLANE)
    gradient = total(parts) * scale
    new_moment = beta_one * moment + (1.0 - beta_one) * gradient
    new_second = beta_two * second_moment + (1.0 - beta_two) * gradient * gradient
    first_fix = 1.0 - beta_one**STEP
    second_fix = 1.0 - beta_two**STEP
    update = (new_moment / first_fix / (jnp.sqrt(new_second / second_fix) + epsilon)).astype(bf16)
    segment = spread(update, PLANE, 16).reshape(rank // 2, width)
    segment = lax.all_gather(segment, "core", axis=0, tiled=True)
    negative = jnp.dot(negative_rows, segment, preferred_element_type=f32)
    new_weight = (weight.astype(f32) + step_size * negative).astype(bf16)
    return (new_weight, new_moment, new_second)


def solution(mesh):
    names = DATA + MODEL
    fine = Mesh(mesh.devices.reshape([SIZES[name] for name in names]), names)
    split = P(DATA, MODEL)
    return jax.shard_map(
        step,
        mesh=fine,
        in_specs=(split, split, P(MODEL, None), split, split, split),
        out_specs=(split, split, split),
        check_vma=False,
    )
```

```python
import math

import jax
import jax.numpy as jnp
from jax import lax
from jax.experimental.layout import Layout, with_layout_constraint
from jax.sharding import Mesh, PartitionSpec as P

STEP = 1000


beta_one = 0.9
beta_two = 0.999
epsilon = 1e-08
step_size = 0.5

DATA = ("zl", "x", "core")
PLANE = ("zl", "x")
MODEL = ("zh", "y")
SIZES = {"zl": 4, "x": 4, "core": 2, "zh": 4, "y": 4}
bf16 = jnp.bfloat16
f32 = jnp.float32


def exchange(parts, axis):
    return lax.all_to_all(parts, axis, 0, 0)


def spread(block, axis, count):
    return exchange(jnp.broadcast_to(block[None], (count,) + block.shape), axis)


def rowwise(array):
    return with_layout_constraint(array, Layout(major_to_minor=(0, 1)))


def total(parts):
    return jnp.sum(parts.astype(f32), axis=0)


NEAR = (((0, 1), (1, 0), (2, 3), (3, 2)), ((0, 3), (3, 0), (1, 2), (2, 1)))


def line_sum(piece, first):
    for stage in range(2):
        other = lax.ppermute(piece, "zh", NEAR[(first + stage) % 2])
        piece = lax.optimization_barrier((piece.astype(f32) + other.astype(f32)).astype(bf16))
    return piece


def regrouped(projector):
    rank = projector.shape[1]
    new = lax.broadcasted_iota(jnp.int32, (rank, rank), 1)
    old = lax.broadcasted_iota(jnp.int32, (rank, rank), 0)
    source = ((new & 240) << 1) | ((new >> 8) << 4) | (new & 15)
    select = (old == source).astype(bf16)
    return jnp.dot(projector, select, preferred_element_type=f32).astype(bf16)


HOPS = ((0, 2, 3, 1), (0, 2, 3, 1), (2, 0, 1, 3), (2, 0, 1, 3))


def place(zl, x, core, zh, y):
    return (((zl * 4 + x) * 2 + core) * 4 + zh) * 4 + y


def moved(rows, source_of):
    pairs = []
    for zl in range(4):
        for x in range(4):
            for core in range(2):
                for zh in range(4):
                    for y in range(4):
                        here = (zl, x, core, zh, y)
                        pairs.append((place(*source_of(*here)), place(*here)))
    return lax.ppermute(rows, DATA + MODEL, pairs)


def basis_rows(half):
    half = moved(half, lambda zl, x, core, zh, y: (zl, x, core, zh, (y - x) % 4))
    half = lax.optimization_barrier(-half)
    return moved(
        half, lambda zl, x, core, zh, y: (HOPS[zl][zh], (y - x) % 4, core, zl, y)
    )


def step(inputs, cotangent, projector, weight, moment, second_moment):
    tokens, width = inputs.shape[0], cotangent.shape[1]
    rank = projector.shape[1]
    rows = weight.shape[0]
    basis = regrouped(projector)
    half = lax.dynamic_slice_in_dim(basis, lax.axis_index("core") * rows, rows, 0)
    basis, half = lax.optimization_barrier((basis, half))
    negative_rows = basis_rows(half)

    partial_sum = rowwise(jnp.dot(inputs, basis, preferred_element_type=f32).astype(bf16))
    parts = exchange(partial_sum.reshape(4, tokens // 4, rank), "y")
    cuts = (0, 9 * (tokens // 64), tokens // 4)
    pieces = []
    for index in range(2):
        piece = parts[:, cuts[index] : cuts[index + 1]]
        piece = lax.optimization_barrier(total(piece).astype(bf16))
        pieces.append(line_sum(piece, index))
    quarter = jnp.concatenate(pieces)
    projected = spread(quarter, "y", 4).reshape(tokens, rank)

    scale = 1.0 / math.sqrt(tokens * 32)
    partial_gradient = lax.dot_general(
        projected, cotangent, (((0,), (0,)), ((), ())), preferred_element_type=f32
    ).astype(bf16)
    parts = exchange(partial_gradient.reshape(2, rank // 2, width), "core")
    chip_gradient = total(parts).astype(bf16)
    parts = exchange(chip_gradient.reshape(16, rank // 32, width), PLANE)
    gradient = total(parts) * scale
    new_moment = beta_one * moment + (1.0 - beta_one) * gradient
    new_second = beta_two * second_moment + (1.0 - beta_two) * gradient * gradient
    first_fix = 1.0 - beta_one**STEP
    second_fix = 1.0 - beta_two**STEP
    update = (new_moment / first_fix / (jnp.sqrt(new_second / second_fix) + epsilon)).astype(bf16)
    segment = spread(update, PLANE, 16).reshape(rank // 2, width)
    segment = lax.all_gather(segment, "core", axis=0, tiled=True)
    negative = jnp.dot(negative_rows, segment, preferred_element_type=f32)
    new_weight = (weight.astype(f32) + step_size * negative).astype(bf16)
    return (new_weight, new_moment, new_second)


def solution(mesh):
    names = DATA + MODEL
    fine = Mesh(mesh.devices.reshape([SIZES[name] for name in names]), names)
    split = P(DATA, MODEL)
    return jax.shard_map(
        step,
        mesh=fine,
        in_specs=(split, split, P(MODEL, None), split, split, split),
        out_specs=(split, split, split),
        check_vma=False,
    )
```

```python
import math

import jax
import jax.numpy as jnp
from jax import lax
from jax.experimental.layout import Layout, with_layout_constraint
from jax.sharding import Mesh, PartitionSpec as P

STEP = 1000


beta_one = 0.9
beta_two = 0.999
epsilon = 1e-08
step_size = 0.5

DATA = ("zl", "x", "core")
PLANE = ("zl", "x")
MODEL = ("zh", "y")
SIZES = {"zl": 4, "x": 4, "core": 2, "zh": 4, "y": 4}
bf16 = jnp.bfloat16
f32 = jnp.float32


def exchange(parts, axis):
    return lax.all_to_all(parts, axis, 0, 0)


def spread(block, axis, count):
    return exchange(jnp.broadcast_to(block[None], (count,) + block.shape), axis)


def rowwise(array):
    return with_layout_constraint(array, Layout(major_to_minor=(0, 1)))


def total(parts):
    return jnp.sum(parts.astype(f32), axis=0)


NEAR = (((0, 1), (1, 0), (2, 3), (3, 2)), ((0, 3), (3, 0), (1, 2), (2, 1)))


def line_sum(piece, first):
    for stage in range(2):
        other = lax.ppermute(piece, "zh", NEAR[(first + stage) % 2])
        piece = lax.optimization_barrier((piece.astype(f32) + other.astype(f32)).astype(bf16))
    return piece


def regrouped(projector):
    rank = projector.shape[1]
    new = lax.broadcasted_iota(jnp.int32, (rank, rank), 1)
    old = lax.broadcasted_iota(jnp.int32, (rank, rank), 0)
    source = ((new & 240) << 1) | ((new >> 8) << 4) | (new & 15)
    select = (old == source).astype(bf16)
    return jnp.dot(projector, select, preferred_element_type=f32).astype(bf16)


HOPS = ((0, 2, 3, 1), (0, 2, 3, 1), (2, 0, 1, 3), (2, 0, 1, 3))


def place(zl, x, core, zh, y):
    return (((zl * 4 + x) * 2 + core) * 4 + zh) * 4 + y


def moved(rows, source_of):
    pairs = []
    for zl in range(4):
        for x in range(4):
            for core in range(2):
                for zh in range(4):
                    for y in range(4):
                        here = (zl, x, core, zh, y)
                        pairs.append((place(*source_of(*here)), place(*here)))
    return lax.ppermute(rows, DATA + MODEL, pairs)


def basis_rows(half):
    half = moved(half, lambda zl, x, core, zh, y: (zl, (y - x) % 4, core, zh, x))
    half = lax.optimization_barrier(-half)
    return moved(
        half, lambda zl, x, core, zh, y: (HOPS[zl][zh], x, core, zl, y)
    )


def step(inputs, cotangent, projector, weight, moment, second_moment):
    tokens, width = inputs.shape[0], cotangent.shape[1]
    rank = projector.shape[1]
    rows = weight.shape[0]
    basis = regrouped(projector)
    half = lax.dynamic_slice_in_dim(basis, lax.axis_index("core") * rows, rows, 0)
    basis, half = lax.optimization_barrier((basis, half))
    negative_rows = basis_rows(half)

    partial_sum = rowwise(jnp.dot(inputs, basis, preferred_element_type=f32).astype(bf16))
    parts = exchange(partial_sum.reshape(4, tokens // 4, rank), "y")
    cuts = (0, 17 * (tokens // 128), tokens // 4)
    pieces = []
    for index in range(2):
        piece = parts[:, cuts[index] : cuts[index + 1]]
        piece = lax.optimization_barrier(total(piece).astype(bf16))
        pieces.append(line_sum(piece, index))
    quarter = jnp.concatenate(pieces)
    projected = spread(quarter, "y", 4).reshape(tokens, rank)

    scale = 1.0 / math.sqrt(tokens * 32)
    partial_gradient = lax.dot_general(
        projected, cotangent, (((0,), (0,)), ((), ())), preferred_element_type=f32
    ).astype(bf16)
    parts = exchange(partial_gradient.reshape(2, rank // 2, width), "core")
    chip_gradient = total(parts).astype(bf16)
    parts = exchange(chip_gradient.reshape(16, rank // 32, width), PLANE)
    gradient = total(parts) * scale
    new_moment = beta_one * moment + (1.0 - beta_one) * gradient
    new_second = beta_two * second_moment + (1.0 - beta_two) * gradient * gradient
    first_fix = 1.0 - beta_one**STEP
    second_fix = 1.0 - beta_two**STEP
    update = (new_moment / first_fix / (jnp.sqrt(new_second / second_fix) + epsilon)).astype(bf16)
    segment = spread(update, PLANE, 16).reshape(rank // 2, width)
    segment = lax.all_gather(segment, "core", axis=0, tiled=True)
    negative = jnp.dot(negative_rows, segment, preferred_element_type=f32)
    new_weight = (weight.astype(f32) + step_size * negative).astype(bf16)
    return (new_weight, new_moment, new_second)


def solution(mesh):
    names = DATA + MODEL
    fine = Mesh(mesh.devices.reshape([SIZES[name] for name in names]), names)
    split = P(DATA, MODEL)
    return jax.shard_map(
        step,
        mesh=fine,
        in_specs=(split, split, P(MODEL, None), split, split, split),
        out_specs=(split, split, split),
        check_vma=False,
    )
```
